256 devices in a mesh: row: 8 (over y_hi, x), col: 32 (over y_lo, z, core).
Axes of the slice: x: 4, y: 4 (y_hi: 2, y_lo: 2; y = y_hi * 2 + y_lo), z: 8, core: 2. Of those that a mesh axis runs over, the one named last changes fastest.
Arguments:
- features: bfloat16 [131072, 128], P(('col', 'row')), may hold values from -6 to 6
- weight: bfloat16 [128, 256], replicated, may hold values from -0.5 to 0.5
- out_grad: bfloat16 [131072, 256], P(('row', 'col')), may hold values from -0.796875 to 0.796875
- tile_index: int32 [8, 32, 64, 3], P('row', 'col'), may hold values from 0 to 127, as said below
- edge_mask: int32 [8, 32, 64, 128, 128], P('row', 'col'), may hold values 0 or 1
- edge_weight: bfloat16 [8, 32, 64, 128, 128], P('row', 'col'), may hold values from 0 to 1
Outputs:
- edge_grad: bfloat16 [8, 32, 64, 128, 128], P('row', 'col')
- feature_grad: bfloat16 [131072, 128], P(('col', 'row'))
The draws below stay inside these ranges and needn't reach their ends.
Inputs may be any that keep to these rules, and one draw needn't show every extreme that they name: `tile_index`: within one device the (tile row, tile column) pairs are distinct; tile rows lie below 128, tile columns below 32; live slots come first, a device has between 21 and 64 of them, and some device has all 64 live.
All inputs are finite; a program needn't handle non-finite values. No bound on the sum of `edge_mask` on one device may be relied on, other than what follows from the above.
Results may differ from the reference program's by a relative error of at most 0.0049.
Values may be sent and summed in bfloat16 or wider, within the bound.
A program may use at most 64 MiB of HBM per device.

```python
import jax
import jax.numpy as jnp
from jax import lax

F = 256
FIN = 128
BLOCK = 128
NODE_DEV = 512
TILES_DEV = 64
NODES = 131072
RB = 128
CB = 32
N_ROW = 8
N_COL = 32


def draw_tile_index(key, part):
    devices = N_ROW * N_COL
    cells = RB * CB
    keys = jax.random.split(jax.random.fold_in(key, 11), devices)
    picks = jax.vmap(lambda sub: jax.random.permutation(sub, cells)[:TILES_DEV])(keys).astype(jnp.int32)
    counts = jax.random.randint(jax.random.fold_in(key, 12), (devices,), TILES_DEV // 3, TILES_DEV + 1)
    fullest = jax.random.randint(jax.random.fold_in(key, 13), (), 0, devices)
    counts = jnp.where(jnp.arange(devices) == fullest, TILES_DEV, counts)
    inner = (jax.random.permutation(jax.random.fold_in(key, 14), cells - 2)[:TILES_DEV - 2] + 1).astype(jnp.int32)
    special = jnp.concatenate([jnp.array([cells - 1, 0], jnp.int32), inner])
    picks = jnp.where((jnp.arange(devices) == fullest)[:, None], special[None, :], picks)
    live = (jnp.arange(TILES_DEV)[None, :] < counts[:, None]).astype(jnp.int32)
    table = jnp.stack([picks // CB, picks % CB, live], axis=-1)
    return table.reshape(N_ROW, N_COL, TILES_DEV, 3).astype(jnp.int32)


def touch_ends(drawn, rng, least, largest):
    extent = drawn.shape
    index_at = [jax.random.randint(jax.random.fold_in(rng, axis), (), 0, extent[axis]) for axis in range(len(extent))]
    drawn = drawn.at[tuple(index_at)].set(least)
    longest = extent.index(max(extent))
    index_at[longest] = (index_at[longest] + 1) % extent[longest]
    return drawn.at[tuple(index_at)].set(largest)


def shard_levels(own_key, shape, cuts, low, high):
    def one(position, shards_of):
        draws = jax.random.uniform(jax.random.fold_in(jax.random.fold_in(own_key, 6), position), (shards_of,), jnp.float32, low / len(cuts), high / len(cuts))
        return jnp.repeat(jnp.exp(draws), shape[position] // shards_of).reshape((-1,) + (1,) * (len(shape) - position - 1))

    factor_of = one(*cuts[0])
    for cut in cuts[1:]:
        factor_of = factor_of * one(*cut)
    return factor_of


def gaussian(rng, extent, spread, most, pieces=(), held_as=jnp.bfloat16):
    drawn = spread * jax.random.normal(rng, extent, jnp.float32)
    if pieces:
        drawn = drawn * shard_levels(rng, extent, pieces, -0.22, 0.18)
    return jnp.clip(drawn, -most, most).astype(held_as)


def setup_inputs(seed: int = 0) -> dict:
    arg_keys = jax.random.split(jax.random.key(seed), 7)
    return {
        "features": gaussian(arg_keys[0], (NODES, FIN), 1.0, 6.0, ((0, 256),)),
        "weight": gaussian(arg_keys[1], (FIN, F), FIN ** -0.5, 0.5),
        "out_grad": gaussian(arg_keys[2], (NODES, F), 0.1, 0.796875, ((0, 256),)),
        "tile_index": draw_tile_index(jax.random.fold_in(arg_keys[6], 71), 0),
        "edge_mask": touch_ends((jax.random.randint(arg_keys[4], (N_ROW, N_COL, TILES_DEV, BLOCK, BLOCK), 0, 4) < 1).astype(jnp.int32), jax.random.fold_in(arg_keys[4], 1), 0, 1),
        "edge_weight": jnp.clip(1.0 * jax.random.uniform(arg_keys[5], (N_ROW, N_COL, TILES_DEV, BLOCK, BLOCK), jnp.float32) ** shard_levels(arg_keys[5], (N_ROW, N_COL, TILES_DEV, BLOCK, BLOCK), ((0, 8), (1, 32)), -0.2, 0.2), 0.0, 1.0).astype(jnp.bfloat16),
    }


def reference(features, weight, out_grad, tile_index, edge_mask, edge_weight):
    proj = jnp.dot(features, weight, preferred_element_type=jnp.float32).astype(jnp.bfloat16)
    row_panel = NODE_DEV * N_COL
    col_panel = NODE_DEV * N_ROW
    flat_index = tile_index.reshape(-1, 3).astype(jnp.int32)
    masks = edge_mask.reshape(-1, BLOCK, BLOCK)
    weights = edge_weight.reshape(-1, BLOCK, BLOCK)
    device = jnp.arange(flat_index.shape[0], dtype=jnp.int32) // TILES_DEV
    row_start = ((device // N_COL) * row_panel + flat_index[:, 0] * BLOCK).astype(jnp.int32)
    col_start = ((device % N_COL) * col_panel + flat_index[:, 1] * BLOCK).astype(jnp.int32)

    def step(total, item):
        rstart, cstart, live, mask_tile, weight_tile = item
        grad_rows = lax.dynamic_slice_in_dim(out_grad, rstart, BLOCK, 0)
        proj_cols = lax.dynamic_slice_in_dim(proj, cstart, BLOCK, 0)
        keep = mask_tile.astype(jnp.float32) * live.astype(jnp.float32)
        scores = jnp.dot(grad_rows, proj_cols.T, preferred_element_type=jnp.float32)
        grad_tile = (keep * scores).astype(jnp.bfloat16)
        adjacency = (weight_tile.astype(jnp.float32) * keep).astype(jnp.bfloat16)
        contrib = jnp.dot(adjacency.T, grad_rows, preferred_element_type=jnp.float32)
        current = lax.dynamic_slice_in_dim(total, cstart, BLOCK, 0)
        total = lax.dynamic_update_slice_in_dim(total, current + contrib, cstart, 0)
        return total, grad_tile

    start_total = jnp.zeros((features.shape[0], out_grad.shape[1]), jnp.float32)
    proj_grad, grads = lax.scan(step, start_total, (row_start, col_start, flat_index[:, 2], masks, weights))
    feature_grad = jnp.dot(proj_grad, weight.astype(jnp.float32).T, precision=lax.Precision.HIGHEST)
    return grads.reshape(edge_mask.shape), feature_grad.astype(jnp.bfloat16)
```

```python
import jax
import jax.numpy as jnp
from jax import lax
from jax.experimental import pallas as pl
from jax.experimental.pallas import tpu as pltpu
from jax.sharding import PartitionSpec as P

BLOCK = 128
STEP = 8


def tiles_kernel(table, grads, feats, mask, weight, edge_grad, partial):
    step = pl.program_id(0)

    @pl.when(step == 0)
    def _():
        partial[...] = jnp.zeros_like(partial)

    for k in range(STEP):
        slot = step * STEP + k
        row, col, live = table[3 * slot], table[3 * slot + 1], table[3 * slot + 2]
        keep = mask[k] * live != 0
        rows = grads[row]
        scores = lax.dot_general(
            rows, feats[col], (((1,), (1,)), ((), ())), preferred_element_type=jnp.float32
        )
        edge_grad[k] = jnp.where(keep, scores, 0.0).astype(jnp.bfloat16)
        adjacency = jnp.where(keep, weight[k].astype(jnp.float32), 0.0).astype(jnp.bfloat16)
        partial[col] += lax.dot_general(
            adjacency, rows, (((0,), (0,)), ((), ())), preferred_element_type=jnp.float32
        )


def tiles(table, grads, feats, mask, weight):
    slots, width = mask.shape[0], grads.shape[-1]
    whole = lambda a: pl.BlockSpec(a.shape, lambda i, t: (0, 0, 0), pipeline_mode=pl.Buffered(1))
    some = pl.BlockSpec((STEP, BLOCK, BLOCK), lambda i, t: (i, 0, 0))
    out = jax.ShapeDtypeStruct(feats.shape, jnp.float32)
    return pl.pallas_call(
        tiles_kernel,
        grid_spec=pltpu.PrefetchScalarGridSpec(
            num_scalar_prefetch=1,
            grid=(slots // STEP,),
            in_specs=[whole(grads), whole(feats), some, some],
            out_specs=[some, pl.BlockSpec(out.shape, lambda i, t: (0, 0, 0))],
        ),
        out_shape=[jax.ShapeDtypeStruct(mask.shape, jnp.bfloat16), out],
        compiler_params=pltpu.CompilerParams(vmem_limit_bytes=32 << 20),
    )(table.reshape(-1), grads, feats, mask, weight)


def local(features, weight, out_grad, tile_index, edge_mask, edge_weight):
    width = features.shape[1]
    folded = lax.dot_general(
        out_grad, weight, (((1,), (1,)), ((), ())), preferred_element_type=jnp.float32
    ).astype(jnp.bfloat16)
    grads = lax.all_gather(folded, "col", axis=0, tiled=True).reshape(-1, BLOCK, width)
    feats = lax.all_gather(features, "row", axis=0, tiled=True).reshape(-1, BLOCK, width)
    edge_grad, partial = tiles(tile_index[0, 0], grads, feats, edge_mask[0, 0], edge_weight[0, 0])
    feature_grad = lax.psum_scatter(
        partial.reshape(-1, width), "row", scatter_dimension=0, tiled=True
    )
    return (edge_grad[None, None], feature_grad.astype(jnp.bfloat16))


def solution(mesh):
    in_specs = (
        P(("col", "row"), None),
        P(),
        P(("row", "col"), None),
        P("row", "col", None, None),
        P("row", "col", None, None, None),
        P("row", "col", None, None, None),
    )
    out_specs = (P("row", "col", None, None, None), P(("col", "row"), None))
    return jax.shard_map(local, mesh=mesh, in_specs=in_specs, out_specs=out_specs, check_vma=False)
```

```python
import jax
import jax.numpy as jnp
from jax import lax
from jax.experimental import pallas as pl
from jax.experimental.pallas import tpu as pltpu
from jax.sharding import PartitionSpec as P

MESH = pl.DeviceIdType.MESH
BLOCK = 128
NX, NZ = 4, 8
CHUNK = 8
F32, BF16 = jnp.float32, jnp.bfloat16


def kernel(
    table,
    table_v,
    out_grad,
    weight,
    features,
    edge_mask,
    edge_weight,
    edge_grad,
    feature_grad,
    hbuf,
    xbuf,
    mask,
    wts,
    adj,
    sums,
    edge_out,
    stage,
    merged,
    relayed,
    landed,
    chain_v,
    chain,
    load_sem,
    out_sem,
    h_send,
    h_recv,
    x_send,
    x_recv,
    g_send,
    g_recv,
):
    slots = mask.shape[0]
    r, c = lax.axis_index("row"), lax.axis_index("col")
    yh, x = r // NX, r % NX
    yl, z, k = c // (2 * NZ), (c // 2) % NZ, c % 2

    def col_of(yl, z, k):
        return (yl * NZ + (z + NZ) % NZ) * 2 + k

    def row_of(yh, x):
        return yh * NX + (x + NX) % NX

    to_z = {s: (r, col_of(yl, z + s, k)) for s in (1, -1)}
    to_y = (r, col_of(1 - yl, z, k))
    to_core = (r, col_of(yl, z, 1 - k))
    to_row = {
        (q, s): (row_of((yh + q) % 2, x + s), c)
        for q in (0, 1)
        for s in (-1, 0, 1)
        if q or s
    }

    loads = [
        pltpu.make_async_copy(features, xbuf.at[pl.ds(4 * r, 4)], load_sem.at[0]),
        pltpu.make_async_copy(edge_mask, mask, load_sem.at[1]),
        pltpu.make_async_copy(edge_weight, wts, load_sem.at[2]),
    ]
    for load in loads:
        load.start()

    barrier = pltpu.get_barrier_semaphore()
    peers = [to_z[1], to_z[-1], to_y, to_core, *to_row.values()]
    for peer in peers:
        pl.semaphore_signal(barrier, inc=1, device_id=peer, device_id_type=MESH)

    folded = lax.dot_general(
        out_grad[...], weight[...], (((1,), (1,)), ((), ())), preferred_element_type=F32
    ).astype(BF16)
    for b in range(4):
        hbuf[4 * c + b] = folded[b * BLOCK : (b + 1) * BLOCK]
    pl.semaphore_wait(barrier, len(peers))

    started = []

    def h_copy(block, half, device, i):
        piece = hbuf.at[pl.ds(4 * block + 2 * half, 2)]
        return pltpu.make_async_remote_copy(
            src_ref=piece,
            dst_ref=piece,
            send_sem=h_send.at[i],
            recv_sem=h_recv.at[2 * block + half],
            device_id=device,
            device_id_type=MESH,
        )

    def put(block, half, device):
        copy = h_copy(block, half, device, len(started))
        copy.start()
        started.append(copy)

    def got(block, half):
        h_copy(block, half, to_core, 0).wait_recv()

    x_started = []

    def x_copy(block, part, n, device, i, sem):
        piece = xbuf.at[pl.ds(4 * block + part, n)]
        return pltpu.make_async_remote_copy(
            src_ref=piece,
            dst_ref=piece,
            send_sem=x_send.at[i],
            recv_sem=x_recv.at[sem],
            device_id=device,
            device_id_type=MESH,
        )

    def x_put(block, part, n, device, sem):
        copy = x_copy(block, part, n, device, len(x_started), sem)
        copy.start()
        x_started.append(copy)

    def x_got(block, part, n, sem):
        x_copy(block, part, n, to_core, 0, sem).wait_recv()

    put(c, 0, to_y)
    put(c, 0, to_z[1])
    put(c, 0, to_z[-1])
    put(c, 1, to_z[1])
    put(c, 1, to_z[-1])
    put(c, 1, to_y)
    put(c, 0, to_core)
    put(c, 1, to_core)
    loads[0].wait()
    x_put(r, 0, 4, to_row[0, 1], 1)
    x_put(r, 0, 4, to_row[0, -1], 2)
    x_put(r, 0, 4, to_row[1, 0], 0)

    cols = table_v[1:2, :]
    wide = jnp.broadcast_to(cols, (slots, slots))
    at_s = lax.broadcasted_iota(jnp.int32, (slots, slots), 0)
    at_q = lax.broadcasted_iota(jnp.int32, (slots, slots), 1)
    tall = jnp.sum(jnp.where(at_s == at_q, wide, 0), axis=1, keepdims=True)
    chain_v[0:1, 0:slots] = jnp.max(
        jnp.where((tall == wide) & (at_s < at_q), at_s, -1), axis=0, keepdims=True
    )
    chain_v[1:2, 0:slots] = jnp.max(jnp.where(tall == at_q, at_s, -1), axis=0, keepdims=True)
    to_scalar = pltpu.make_async_copy(chain_v, chain, load_sem.at[3])
    to_scalar.start()

    loads[1].wait()
    loads[2].wait()

    def prepare(first, n):
        def one(t, carry):
            keep = mask[t] * table[2, t] != 0
            kept = jnp.where(keep, wts[t].astype(F32), 0.0)
            adj[t] = kept.T.astype(BF16)
            return carry

        lax.fori_loop(first, first + n, one, 0, unroll=2)

    mate = col_of(1 - yl, z, k)
    got(mate, 0)
    put(mate, 0, to_z[1])
    put(mate, 0, to_z[-1])
    put(mate, 0, to_core)
    prepare(0, 8)

    done = 8
    for s in range(1, 4):
        for sign in (1, -1):
            near = col_of(yl, z - sign * s, k)
            far = col_of(1 - yl, z - sign * s, k)
            for half in (0, 1):
                got(near, half)
                if s < 3 or half == (0 if sign > 0 else 1):
                    put(near, half, to_z[sign])
                if half:
                    put(near, half, to_y)
                put(near, half, to_core)
            got(far, 0)
            if s < 3:
                put(far, 0, to_z[sign])
            put(far, 0, to_core)
        if s == 3:
            way = 1 - 2 * k
            put(col_of(1 - yl, z - 3 * way, k), 0, (r, col_of(yl, z + way, k)))
        for back in (s - 1,) if s == 1 else (s - 1, 1 - s):
            late = col_of(1 - yl, z + back, k)
            got(late, 1)
            put(late, 1, to_core)
        if s == 1:
            other = row_of(1 - yh, x)
            x_got(other, 0, 4, 0)
            x_put(other, 0, 4, to_row[0, 1], 3)
            x_put(other, 0, 4, to_row[0, -1], 4)
        if s == 2:
            left, right = row_of(yh, x - 1), row_of(yh, x + 1)
            x_got(left, 0, 4, 1)
            x_put(left, 0, 2, to_row[0, 1], 5)
            x_got(right, 0, 4, 2)
            x_put(right, 2, 2, to_row[0, -1], 6)
        if s == 3:
            left, right = row_of(1 - yh, x - 1), row_of(1 - yh, x + 1)
            x_got(left, 0, 4, 3)
            x_put(left, 0, 2, to_row[0, 1], 7)
            x_got(right, 0, 4, 4)
            x_put(right, 2, 2, to_row[0, -1], 8)
        more = 24 if s < 3 else slots - done
        if more:
            prepare(done, more)
        done += more
    near, far = col_of(yl, z + 4, k), col_of(1 - yl, z + 4, k)
    got(near, 1)
    put(near, 1, to_y)
    put(near, 1, to_core)
    got(near, 0)
    put(near, 0, to_core)
    got(far, 0)
    put(far, 0, to_core)
    for s in (3, -3, 4):
        late = col_of(1 - yl, z + s, k)
        got(late, 1)
        put(late, 1, to_core)

    def from_core(i, carry):
        got(2 * i + 1 - k, 0)
        got(2 * i + 1 - k, 1)
        return carry

    lax.fori_loop(0, 2 * NZ, from_core, 0)
    to_scalar.wait()

    def add(t, carry):
        before = chain[0, t]
        part = jnp.dot(adj[t], hbuf[table[0, t]], preferred_element_type=F32)
        sums[t] = part + jnp.where(before >= 0, sums[jnp.maximum(before, 0)], 0.0)
        return carry

    lax.fori_loop(0, slots, add, 0, unroll=4)

    def total(block):
        final = chain[1, block]
        return jnp.where(final >= 0, sums[jnp.maximum(final, 0)], 0.0)

    def fill(dest, first, n):
        for b in range(first, first + n):
            stage[4 * dest + b] = total(4 * dest + b).astype(BF16)

    g_started = []

    def g_put(src, dst, sem, device):
        copy = pltpu.make_async_remote_copy(
            src_ref=src,
            dst_ref=dst,
            send_sem=g_send.at[len(g_started)],
            recv_sem=g_recv.at[sem],
            device_id=device,
            device_id_type=MESH,
        )
        copy.start()
        g_started.append(copy)

    def g_got(dst, sem):
        pltpu.make_async_remote_copy(
            src_ref=dst,
            dst_ref=dst,
            send_sem=g_send.at[0],
            recv_sem=g_recv.at[sem],
            device_id=to_core,
            device_id_type=MESH,
        ).wait_recv()

    sides = ((1, 0), (-1, 1))
    for q in (0, 1):
        dest = row_of((yh + q) % 2, x + 2)
        fill(dest, 0, 4)
        for s, half in sides:
            i = 2 * q + half
            g_put(
                stage.at[pl.ds(4 * dest + 2 * half, 2)],
                relayed.at[pl.ds(2 * i, 2)],
                i,
                to_row[0, s],
            )
    for q in (1, 0):
        for s, half in sides:
            dest = row_of((yh + q) % 2, x + s)
            fill(dest, 0, 4)
            i = 2 * q + half
            plain = 1 - half
            g_put(
                stage.at[pl.ds(4 * dest + 2 * plain, 2)],
                landed.at[pl.ds(4 * i + 2 * plain, 2)],
                4 + 2 * i + plain,
                to_row[q, s],
            )
    dest = row_of(1 - yh, x)
    fill(dest, 0, 4)
    g_put(stage.at[pl.ds(4 * dest, 4)], landed.at[pl.ds(16, 4)], 12, to_row[1, 0])
    for q in (1, 0):
        for s, half in sides:
            dest = row_of((yh + q) % 2, x + s)
            i = 2 * q + half
            g_got(relayed.at[pl.ds(2 * i, 2)], i)
            for b in (0, 1):
                merged[2 * i + b] = (
                    total(4 * dest + 2 * half + b) + relayed[2 * i + b].astype(F32)
                ).astype(BF16)
            g_put(
                merged.at[pl.ds(2 * i, 2)],
                landed.at[pl.ds(4 * i + 2 * half, 2)],
                4 + 2 * i + half,
                to_row[q, s],
            )

    far_x = row_of(yh, x + 2)
    x_got(far_x, 0, 2, 5)
    x_got(far_x, 2, 2, 6)
    far_x = row_of(1 - yh, x + 2)
    x_got(far_x, 0, 2, 7)
    x_got(far_x, 2, 2, 8)

    def chunk_out(i):
        part = pl.ds(i * CHUNK, CHUNK)
        return pltpu.make_async_copy(edge_out.at[part], edge_grad.at[part], out_sem.at[i])

    def chunk(i, carry):
        for j in range(CHUNK):
            t = i * CHUNK + j
            keep = mask[t] * table[2, t] != 0
            scores = lax.dot_general(
                hbuf[table[0, t]],
                xbuf[table[1, t]],
                (((1,), (1,)), ((), ())),
                preferred_element_type=F32,
            )
            edge_out[t] = jnp.where(keep, scores, 0.0).astype(BF16)
        chunk_out(i).start()
        return carry

    lax.fori_loop(0, slots // CHUNK, chunk, 0)

    for i in range(4):
        for half in (0, 1):
            g_got(landed.at[pl.ds(4 * i + 2 * half, 2)], 4 + 2 * i + half)
    g_got(landed.at[pl.ds(16, 4)], 12)
    for b in range(4):
        value = total(4 * r + b)
        for i in range(5):
            value += landed[4 * i + b].astype(F32)
        feature_grad[b] = value.astype(BF16)

    for copy in started + x_started + g_started:
        copy.wait_send()
    for i in range(slots // CHUNK):
        chunk_out(i).wait()


def local(features, weight, out_grad, tile_index, edge_mask, edge_weight):
    nodes, width = features.shape
    slots = edge_mask.shape[2]
    table = tile_index[0, 0].T
    blocks = nodes // BLOCK
    vmem = pl.BlockSpec(memory_space=pltpu.VMEM)
    hbm = pl.BlockSpec(memory_space=pl.ANY)
    dma = pltpu.SemaphoreType.DMA
    tile = (BLOCK, BLOCK)
    edge_grad, feature_grad = pl.pallas_call(
        kernel,
        in_specs=[pl.BlockSpec(memory_space=pltpu.SMEM), vmem, vmem, vmem, hbm, hbm, hbm],
        out_specs=[hbm, vmem],
        out_shape=[
            jax.ShapeDtypeStruct((slots, *tile), BF16),
            jax.ShapeDtypeStruct((blocks, *tile), BF16),
        ],
        scratch_shapes=[
            pltpu.VMEM((4 * blocks * NZ, *tile), BF16),
            pltpu.VMEM((2 * blocks * NX, *tile), BF16),
            pltpu.VMEM((slots, *tile), jnp.int32),
            pltpu.VMEM((slots, *tile), BF16),
            pltpu.VMEM((slots, *tile), BF16),
            pltpu.VMEM((slots, *tile), F32),
            pltpu.VMEM((slots, *tile), BF16),
            pltpu.VMEM((2 * blocks * NX, *tile), BF16),
            pltpu.VMEM((8, *tile), BF16),
            pltpu.VMEM((8, *tile), BF16),
            pltpu.VMEM((20, *tile), BF16),
            pltpu.VMEM((8, 128), jnp.int32),
            pltpu.SMEM((8, 128), jnp.int32),
            dma((4,)),
            dma((slots // CHUNK,)),
            dma((62,)),
            dma((64,)),
            dma((9,)),
            dma((9,)),
            dma((13,)),
            dma((13,)),
        ],
        compiler_params=pltpu.CompilerParams(
            collective_id=0, has_side_effects=True, vmem_limit_bytes=56 << 20
        ),
        name="layer",
    )(
        table,
        table,
        out_grad,
        weight,
        features.reshape(blocks, *tile),
        edge_mask[0, 0],
        edge_weight[0, 0],
    )
    return (edge_grad[None, None], feature_grad.reshape(nodes, width))


def solution(mesh):
    in_specs = (
        P(("col", "row"), None),
        P(),
        P(("row", "col"), None),
        P("row", "col", None, None),
        P("row", "col", None, None, None),
        P("row", "col", None, None, None),
    )
    out_specs = (P("row", "col", None, None, None), P(("col", "row"), None))
    return jax.shard_map(local, mesh=mesh, in_specs=in_specs, out_specs=out_specs, check_vma=False)
```

```python
import jax
import jax.numpy as jnp
from jax import lax
from jax.experimental import pallas as pl
from jax.experimental.pallas import tpu as pltpu
from jax.sharding import PartitionSpec as P

MESH = pl.DeviceIdType.MESH
BLOCK = 128
NX, NZ = 4, 8
CHUNK = 8
F32, BF16 = jnp.float32, jnp.bfloat16


def kernel(
    table,
    table_v,
    out_grad,
    weight,
    features,
    edge_mask,
    edge_weight,
    edge_grad,
    feature_grad,
    hbuf,
    xbuf,
    mask,
    wts,
    adj,
    sums,
    stage,
    merged,
    relayed,
    landed,
    chain_v,
    chain,
    load_sem,
    h_send,
    h_recv,
    x_send,
    x_recv,
    g_send,
    g_recv,
):
    slots = mask.shape[0]
    r, c = lax.axis_index("row"), lax.axis_index("col")
    yh, x = r // NX, r % NX
    yl, z, k = c // (2 * NZ), (c // 2) % NZ, c % 2

    def col_of(yl, z, k):
        return (yl * NZ + (z + NZ) % NZ) * 2 + k

    def row_of(yh, x):
        return yh * NX + (x + NX) % NX

    to_z = {s: (r, col_of(yl, z + s, k)) for s in (1, -1)}
    to_y = (r, col_of(1 - yl, z, k))
    to_core = (r, col_of(yl, z, 1 - k))
    to_row = {
        (q, s): (row_of((yh + q) % 2, x + s), c)
        for q in (0, 1)
        for s in (-1, 0, 1)
        if q or s
    }

    loads = [
        pltpu.make_async_copy(features, xbuf.at[pl.ds(4 * r, 4)], load_sem.at[0]),
        pltpu.make_async_copy(edge_mask, mask, load_sem.at[1]),
        pltpu.make_async_copy(edge_weight, wts, load_sem.at[2]),
    ]
    for load in loads:
        load.start()

    barrier = pltpu.get_barrier_semaphore()
    peers = [to_z[1], to_z[-1], to_y, to_core, *to_row.values()]
    for peer in peers:
        pl.semaphore_signal(barrier, inc=1, device_id=peer, device_id_type=MESH)

    folded = lax.dot_general(
        out_grad[...], weight[...], (((1,), (1,)), ((), ())), preferred_element_type=F32
    ).astype(BF16)
    for b in range(4):
        hbuf[4 * c + b] = folded[b * BLOCK : (b + 1) * BLOCK]
    pl.semaphore_wait(barrier, len(peers))

    started = []

    def h_copy(block, half, device, i):
        piece = hbuf.at[pl.ds(4 * block + 2 * half, 2)]
        return pltpu.make_async_remote_copy(
            src_ref=piece,
            dst_ref=piece,
            send_sem=h_send.at[i],
            recv_sem=h_recv.at[2 * block + half],
            device_id=device,
            device_id_type=MESH,
        )

    def put(block, half, device):
        copy = h_copy(block, half, device, len(started))
        copy.start()
        started.append(copy)

    def got(block, half):
        h_copy(block, half, to_core, 0).wait_recv()

    x_started = []

    def x_copy(block, part, n, device, i, sem):
        piece = xbuf.at[pl.ds(4 * block + part, n)]
        return pltpu.make_async_remote_copy(
            src_ref=piece,
            dst_ref=piece,
            send_sem=x_send.at[i],
            recv_sem=x_recv.at[sem],
            device_id=device,
            device_id_type=MESH,
        )

    def x_put(block, part, n, device, sem):
        copy = x_copy(block, part, n, device, len(x_started), sem)
        copy.start()
        x_started.append(copy)

    def x_got(block, part, n, sem):
        x_copy(block, part, n, to_core, 0, sem).wait_recv()

    put(c, 0, to_y)
    for half in (1, 0):
        for sign in (1, -1):
            put(c, half, to_z[sign])
        if half:
            put(c, half, to_y)
    put(c, 1, to_core)
    put(c, 0, to_core)
    loads[0].wait()
    x_put(r, 0, 4, to_row[0, 1], 1)
    x_put(r, 0, 4, to_row[0, -1], 2)
    x_put(r, 0, 4, to_row[1, 0], 0)

    cols = table_v[1]
    wide = jnp.broadcast_to(cols, (slots, slots))
    at_s = lax.broadcasted_iota(jnp.int32, (slots, slots), 0)
    at_q = lax.broadcasted_iota(jnp.int32, (slots, slots), 1)
    tall = jnp.sum(jnp.where(at_s == at_q, wide, 0), axis=1, keepdims=True)
    chain_v[0:1, 0:slots] = jnp.max(
        jnp.where((tall == wide) & (at_s < at_q), at_s, -1), axis=0, keepdims=True
    )
    chain_v[1:2, 0:slots] = jnp.max(jnp.where(tall == at_q, at_s, -1), axis=0, keepdims=True)
    to_scalar = pltpu.make_async_copy(chain_v, chain, load_sem.at[3])
    to_scalar.start()

    loads[1].wait()
    loads[2].wait()

    def prepare(first, n):
        def one(t, carry):
            keep = mask[t] * table[2, 0, t] != 0
            kept = jnp.where(keep, wts[t].astype(F32), 0.0)
            adj[t] = kept.T.astype(BF16)
            return carry

        lax.fori_loop(first, first + n, one, 0, unroll=2)

    mate = col_of(1 - yl, z, k)
    got(mate, 0)
    put(mate, 0, to_z[1])
    put(mate, 0, to_z[-1])
    put(mate, 0, to_core)
    prepare(0, 8)

    done = 8
    for s in range(1, 4):
        near = {sign: col_of(yl, z - sign * s, k) for sign in (1, -1)}
        far = {sign: col_of(1 - yl, z - sign * s, k) for sign in (1, -1)}
        for half in (1, 0):
            for sign in (1, -1):
                got(near[sign], half)
                if s < 3 or half == (0 if sign > 0 else 1):
                    put(near[sign], half, to_z[sign])
                if half:
                    put(near[sign], half, to_y)
                put(near[sign], half, to_core)
        for sign in (1, -1):
            got(far[sign], 0)
            if s < 3:
                put(far[sign], 0, to_z[sign])
            put(far[sign], 0, to_core)
        if s == 3:
            way = 1 - 2 * k
            put(col_of(1 - yl, z - 3 * way, k), 0, (r, col_of(yl, z + way, k)))
        for back in (s - 1,) if s == 1 else (s - 1, 1 - s):
            late = col_of(1 - yl, z + back, k)
            got(late, 1)
            put(late, 1, to_core)
        if s == 1:
            other = row_of(1 - yh, x)
            x_got(other, 0, 4, 0)
            x_put(other, 0, 4, to_row[0, 1], 3)
            x_put(other, 0, 4, to_row[0, -1], 4)
        if s == 2:
            left, right = row_of(yh, x - 1), row_of(yh, x + 1)
            x_got(left, 0, 4, 1)
            x_put(left, 0, 2, to_row[0, 1], 5)
            x_got(right, 0, 4, 2)
            x_put(right, 2, 2, to_row[0, -1], 6)
        if s == 3:
            left, right = row_of(1 - yh, x - 1), row_of(1 - yh, x + 1)
            x_got(left, 0, 4, 3)
            x_put(left, 0, 2, to_row[0, 1], 7)
            x_got(right, 0, 4, 4)
            x_put(right, 2, 2, to_row[0, -1], 8)
        more = 24 if s < 3 else slots - done
        if more:
            prepare(done, more)
        done += more
    near, far = col_of(yl, z + 4, k), col_of(1 - yl, z + 4, k)
    got(near, 1)
    put(near, 1, to_y)
    put(near, 1, to_core)
    got(near, 0)
    put(near, 0, to_core)
    got(far, 0)
    put(far, 0, to_core)
    for s in (3, -3, 4):
        late = col_of(1 - yl, z + s, k)
        got(late, 1)
        put(late, 1, to_core)

    def from_core(i, carry):
        got(2 * i + 1 - k, 0)
        got(2 * i + 1 - k, 1)
        return carry

    lax.fori_loop(0, 2 * NZ, from_core, 0)
    to_scalar.wait()

    def add(t, carry):
        before = chain[0, t]
        part = jnp.dot(adj[t], hbuf[table[0, 0, t]], preferred_element_type=F32)
        sums[t] = part + jnp.where(before >= 0, sums[jnp.maximum(before, 0)], 0.0)
        return carry

    lax.fori_loop(0, slots, add, 0, unroll=16)

    def total(block):
        final = chain[1, block]
        return jnp.where(final >= 0, sums[jnp.maximum(final, 0)], 0.0)

    def fill(dest, first, n):
        for b in range(first, first + n):
            stage[4 * dest + b] = total(4 * dest + b).astype(BF16)

    g_started = []

    def g_put(src, dst, sem, device):
        copy = pltpu.make_async_remote_copy(
            src_ref=src,
            dst_ref=dst,
            send_sem=g_send.at[len(g_started)],
            recv_sem=g_recv.at[sem],
            device_id=device,
            device_id_type=MESH,
        )
        copy.start()
        g_started.append(copy)

    def g_got(dst, sem):
        pltpu.make_async_remote_copy(
            src_ref=dst,
            dst_ref=dst,
            send_sem=g_send.at[0],
            recv_sem=g_recv.at[sem],
            device_id=to_core,
            device_id_type=MESH,
        ).wait_recv()

    sides = ((1, 0), (-1, 1))
    for q in (0, 1):
        dest = row_of((yh + q) % 2, x + 2)
        fill(dest, 0, 4)
        for s, half in sides:
            i = 2 * q + half
            g_put(
                stage.at[pl.ds(4 * dest + 2 * half, 2)],
                relayed.at[pl.ds(2 * i, 2)],
                i,
                to_row[0, s],
            )
    for q in (1, 0):
        for s, half in sides:
            dest = row_of((yh + q) % 2, x + s)
            fill(dest, 0, 4)
            i = 2 * q + half
            plain = 1 - half
            g_put(
                stage.at[pl.ds(4 * dest + 2 * plain, 2)],
                landed.at[pl.ds(4 * i + 2 * plain, 2)],
                4 + 2 * i + plain,
                to_row[q, s],
            )
    dest = row_of(1 - yh, x)
    fill(dest, 0, 4)
    g_put(stage.at[pl.ds(4 * dest, 4)], landed.at[pl.ds(16, 4)], 12, to_row[1, 0])
    for q in (1, 0):
        for s, half in sides:
            dest = row_of((yh + q) % 2, x + s)
            i = 2 * q + half
            g_got(relayed.at[pl.ds(2 * i, 2)], i)
            for b in (0, 1):
                merged[2 * i + b] = (
                    total(4 * dest + 2 * half + b) + relayed[2 * i + b].astype(F32)
                ).astype(BF16)
            g_put(
                merged.at[pl.ds(2 * i, 2)],
                landed.at[pl.ds(4 * i + 2 * half, 2)],
                4 + 2 * i + half,
                to_row[q, s],
            )

    far_x = row_of(yh, x + 2)
    x_got(far_x, 0, 2, 5)
    x_got(far_x, 2, 2, 6)
    far_x = row_of(1 - yh, x + 2)
    x_got(far_x, 0, 2, 7)
    x_got(far_x, 2, 2, 8)

    def chunk(i, carry):
        for j in range(CHUNK):
            t = i * CHUNK + j
            keep = mask[t] * table[2, 0, t] != 0
            scores = lax.dot_general(
                hbuf[table[0, 0, t]],
                xbuf[table[1, 0, t]],
                (((1,), (1,)), ((), ())),
                preferred_element_type=F32,
            )
            edge_grad[t] = jnp.where(keep, scores, 0.0).astype(BF16)
        return carry

    lax.fori_loop(0, slots // CHUNK, chunk, 0)

    for i in range(4):
        for half in (0, 1):
            g_got(landed.at[pl.ds(4 * i + 2 * half, 2)], 4 + 2 * i + half)
    g_got(landed.at[pl.ds(16, 4)], 12)
    for b in range(4):
        value = total(4 * r + b)
        for i in range(5):
            value += landed[4 * i + b].astype(F32)
        feature_grad[b] = value.astype(BF16)

    for copy in started + x_started + g_started:
        copy.wait_send()


def local(features, weight, out_grad, tile_index, edge_mask, edge_weight):
    nodes, width = features.shape
    slots = edge_mask.shape[2]
    table = tile_index[0].transpose(2, 0, 1)
    blocks = nodes // BLOCK
    vmem = pl.BlockSpec(memory_space=pltpu.VMEM)
    hbm = pl.BlockSpec(memory_space=pl.ANY)
    dma = pltpu.SemaphoreType.DMA
    tile = (BLOCK, BLOCK)
    edge_grad, feature_grad = pl.pallas_call(
        kernel,
        in_specs=[pl.BlockSpec(memory_space=pltpu.SMEM), vmem, vmem, vmem, hbm, hbm, hbm],
        out_specs=[vmem, vmem],
        out_shape=[
            pltpu.VMEM((slots, *tile), BF16),
            pltpu.VMEM((blocks, *tile), BF16),
        ],
        scratch_shapes=[
            pltpu.VMEM((4 * blocks * NZ, *tile), BF16),
            pltpu.VMEM((2 * blocks * NX, *tile), BF16),
            pltpu.VMEM((slots, *tile), jnp.int32),
            pltpu.VMEM((slots, *tile), BF16),
            pltpu.VMEM((slots, *tile), BF16),
            pltpu.VMEM((slots, *tile), F32),
            pltpu.VMEM((2 * blocks * NX, *tile), BF16),
            pltpu.VMEM((8, *tile), BF16),
            pltpu.VMEM((8, *tile), BF16),
            pltpu.VMEM((20, *tile), BF16),
            pltpu.VMEM((8, 128), jnp.int32),
            pltpu.SMEM((8, 128), jnp.int32),
            dma((4,)),
            dma((62,)),
            dma((64,)),
            dma((9,)),
            dma((9,)),
            dma((13,)),
            dma((13,)),
        ],
        compiler_params=pltpu.CompilerParams(
            collective_id=0, has_side_effects=True, vmem_limit_bytes=56 << 20
        ),
        name="layer",
    )(
        table,
        table,
        out_grad,
        weight,
        features.reshape(blocks, *tile),
        edge_mask[0, 0],
        edge_weight[0, 0],
    )
    return (edge_grad[None, None], feature_grad.reshape(nodes, width))


def solution(mesh):
    in_specs = (
        P(("col", "row"), None),
        P(),
        P(("row", "col"), None),
        P("row", "col", None, None),
        P("row", "col", None, None, None),
        P("row", "col", None, None, None),
    )
    out_specs = (P("row", "col", None, None, None), P(("col", "row"), None))
    return jax.shard_map(local, mesh=mesh, in_specs=in_specs, out_specs=out_specs, check_vma=False)
```

```python
import jax
import jax.numpy as jnp
from jax import lax
from jax.experimental import pallas as pl
from jax.experimental.pallas import tpu as pltpu
from jax.sharding import PartitionSpec as P

MESH = pl.DeviceIdType.MESH
BLOCK = 128
NX, NZ = 4, 8
CHUNK, GROUP = 8, 16
F32, BF16 = jnp.float32, jnp.bfloat16
RIDE, POST = (0, 1), (2, 3)


def kernel(
    table,
    table_v,
    out_grad,
    weight,
    features,
    edge_mask,
    edge_weight,
    edge_grad,
    feature_grad,
    hbuf,
    xbuf,
    mask,
    wts,
    adj,
    sums,
    stage,
    merged,
    relayed,
    landed,
    order_v,
    order,
    load_sem,
    h_send,
    h_recv,
    x_send,
    x_recv,
    g_send,
    g_recv,
):
    slots = mask.shape[0]
    r, c = lax.axis_index("row"), lax.axis_index("col")
    yh, x = r // NX, r % NX
    yl, z, k = c // (2 * NZ), (c // 2) % NZ, c % 2

    def col_of(yl, z, k):
        return (yl * NZ + (z + NZ) % NZ) * 2 + k

    def row_of(yh, x):
        return yh * NX + (x + NX) % NX

    to_z = {s: (r, col_of(yl, z + s, k)) for s in (1, -1)}
    to_y = (r, col_of(1 - yl, z, k))
    to_core = (r, col_of(yl, z, 1 - k))
    to_row = {
        (q, s): (row_of((yh + q) % 2, x + s), c)
        for q in (0, 1)
        for s in (-1, 0, 1)
        if q or s
    }

    loads = [
        pltpu.make_async_copy(src, dst, load_sem.at[i])
        for i, (src, dst) in enumerate(
            ((features, xbuf.at[pl.ds(4 * r, 4)]), (edge_mask, mask), (edge_weight, wts))
        )
    ]
    for load in loads:
        load.start()

    barrier = pltpu.get_barrier_semaphore()
    peers = [to_z[1], to_z[-1], to_y, to_core, *to_row.values()]
    for peer in peers:
        pl.semaphore_signal(barrier, inc=1, device_id=peer, device_id_type=MESH)

    folded = lax.dot_general(
        out_grad[...], weight[...], (((1,), (1,)), ((), ())), preferred_element_type=F32
    ).astype(BF16)
    for b in range(4):
        hbuf[4 * c + b] = folded[b * BLOCK : (b + 1) * BLOCK]
    pl.semaphore_wait(barrier, len(peers))

    def remote(src, dst, send_sem, recv_sem, device):
        return pltpu.make_async_remote_copy(
            src_ref=src,
            dst_ref=dst,
            send_sem=send_sem,
            recv_sem=recv_sem,
            device_id=device,
            device_id_type=MESH,
        )

    names = [("mate", b) for b in RIDE]
    names += [("near", s, sign, b) for s in (1, 2, 3) for sign in (1, -1) for b in (*POST, *RIDE)]
    names += [("near", 4, 1, b) for b in (*POST, *RIDE)]
    names += [("far", s, sign, b) for s in (1, 2, 3) for sign in (1, -1) for b in RIDE]
    names += [("far", 4, 1, b) for b in RIDE]
    names += [("late", s) for s in (0, 1, -1, 2, -2, 3, -3, 4)]
    names += [("core",)]
    h_sem = {name: i for i, name in enumerate(names)}

    sent = []

    def put(block, first, n, device, *name):
        piece = hbuf.at[pl.ds(4 * block + first, n)]
        remote(piece, piece, h_send.at[0], h_recv.at[h_sem[name]], device).start()
        sent.append(n)

    def got(block, first, n, *name):
        piece = hbuf.at[pl.ds(4 * block + first, n)]
        remote(piece, piece, h_send.at[0], h_recv.at[h_sem[name]], to_core).wait_recv()

    def put_core(block):
        put(block, 0, 4, to_core, "core")

    def x_put(block, first, n, device, sem):
        piece = xbuf.at[pl.ds(4 * block + first, n)]
        remote(piece, piece, x_send.at[0], x_recv.at[sem], device).start()

    def x_got(block, first, n, sem):
        piece = xbuf.at[pl.ds(4 * block + first, n)]
        remote(piece, piece, x_send.at[0], x_recv.at[sem], to_core).wait_recv()

    for b in RIDE:
        put(c, b, 1, to_y, "mate", b)
    for b in (*POST, *RIDE):
        for sign in (1, -1):
            put(c, b, 1, to_z[sign], "near", 1, sign, b)
    for b in POST:
        put(c, b, 1, to_y, "late", 0)
    put_core(c)
    loads[0].wait()
    x_put(r, 0, 4, to_row[0, 1], 1)
    x_put(r, 0, 4, to_row[0, -1], 2)

    square = (slots, slots)
    at_s = lax.broadcasted_iota(jnp.int32, square, 0)
    at_q = lax.broadcasted_iota(jnp.int32, square, 1)

    def upright(line):
        return jnp.sum(
            jnp.where(at_s == at_q, jnp.broadcast_to(line, square), 0), axis=1, keepdims=True
        )

    def gather(where, column):
        return jnp.sum(jnp.where(where, column, 0), axis=0, keepdims=True)

    cols = jnp.broadcast_to(table_v[1], square)
    col_up, row_up = upright(table_v[1]), upright(table_v[0])
    before = cols * slots + at_q < col_up * slots + at_s
    rank = jnp.sum(jnp.where(before, 1, 0), axis=1, keepdims=True)
    here = rank == at_q
    col_here = gather(here, col_up)
    col_before = gather(rank == at_q - 1, col_up)
    first_lane = at_q[0:1] == 0
    order_v[0:1, 0:slots] = gather(here, at_s)
    order_v[1:2, 0:slots] = gather(here, row_up)
    order_v[2:3, 0:slots] = jnp.where((col_here == col_before) & ~first_lane, 1, 0)
    order_v[3:4, 0:slots] = jnp.where(
        gather(col_up == at_q, 1) > 0, gather(col_up <= at_q, 1) - 1, -1
    )
    to_scalar = pltpu.make_async_copy(order_v, order, load_sem.at[3])
    to_scalar.start()
    mate = col_of(1 - yl, z, k)
    for b in RIDE:
        got(mate, b, 1, "mate", b)
        for sign in (1, -1):
            put(mate, b, 1, to_z[sign], "far", 1, sign, b)
    to_scalar.wait()
    loads[1].wait()
    loads[2].wait()

    def prepare(first, n):
        def one(i, carry):
            t = order[0, i]
            keep = mask[t] * table[2, 0, t] != 0
            kept = jnp.where(keep, wts[t].astype(F32), 0.0)
            adj[i] = kept.T.astype(BF16)
            return carry

        lax.fori_loop(first, first + n, one, 0, unroll=2)

    def late(s):
        block = col_of(1 - yl, z + s, k)
        got(block, 2, 2, "late", s)
        put_core(block)

    prepare(0, 8)
    done = 8
    for s in (1, 2, 3):
        near = {sign: col_of(yl, z - sign * s, k) for sign in (1, -1)}
        far = {sign: col_of(1 - yl, z - sign * s, k) for sign in (1, -1)}
        for b in (*POST, *RIDE):
            for sign in (1, -1):
                got(near[sign], b, 1, "near", s, sign, b)
                if s < 3:
                    put(near[sign], b, 1, to_z[sign], "near", s + 1, sign, b)
                elif b in (RIDE if sign > 0 else POST):
                    put(near[sign], b, 1, to_z[sign], "near", 4, 1, b)
                if b in POST:
                    put(near[sign], b, 1, to_y, "late", -sign * s)
        for sign in (1, -1):
            put_core(near[sign])
        for b in RIDE:
            for sign in (1, -1):
                got(far[sign], b, 1, "far", s, sign, b)
                if s < 3:
                    put(far[sign], b, 1, to_z[sign], "far", s + 1, sign, b)
            if s == 3:
                way = 1 - 2 * k
                put(
                    col_of(1 - yl, z - 3 * way, k),
                    b,
                    1,
                    (r, col_of(yl, z + way, k)),
                    "far",
                    4,
                    1,
                    b,
                )
        for back in (s - 1,) if s == 1 else (s - 1, 1 - s):
            late(back)
        if s == 1:
            x_put(r, 0, 4, to_row[1, 0], 0)
        if s == 2:
            left, right = row_of(yh, x - 1), row_of(yh, x + 1)
            x_got(left, 0, 4, 1)
            x_put(left, 0, 2, to_row[0, 1], 5)
            x_got(right, 0, 4, 2)
            x_put(right, 2, 2, to_row[0, -1], 5)
        if s == 3:
            other = row_of(1 - yh, x)
            x_got(other, 0, 4, 0)
            x_put(other, 0, 4, to_row[0, 1], 3)
            x_put(other, 0, 4, to_row[0, -1], 4)
        more = 24 if s < 3 else slots - done
        if more:
            prepare(done, more)
        done += more
    near, far = col_of(yl, z + 4, k), col_of(1 - yl, z + 4, k)
    for b in POST:
        got(near, b, 1, "near", 4, 1, b)
        put(near, b, 1, to_y, "late", 4)
    for b in RIDE:
        got(near, b, 1, "near", 4, 1, b)
    put_core(near)
    for b in RIDE:
        got(far, b, 1, "far", 4, 1, b)
    for s in (3, -3, 4):
        late(s)
    left, right = row_of(1 - yh, x - 1), row_of(1 - yh, x + 1)
    x_got(left, 0, 4, 3)
    x_put(left, 0, 2, to_row[0, 1], 5)
    x_got(right, 0, 4, 4)
    x_put(right, 2, 2, to_row[0, -1], 5)
    got(0, 0, 8 * NZ, "core")

    def group(g, carry):
        run = sums[g * GROUP]
        for j in range(GROUP):
            i = g * GROUP + j
            added = jnp.dot(adj[i], hbuf[order[1, i]], preferred_element_type=F32)
            run = added + jnp.where(order[2, i] != 0, run, 0.0)
            sums[i + 1] = run
        return carry

    sums[0] = jnp.zeros((BLOCK, BLOCK), F32)
    lax.fori_loop(0, slots // GROUP, group, 0)

    def total(block):
        at = order[3, block]
        return jnp.where(at >= 0, sums[at + 1], 0.0)

    def fill(dest):
        for b in range(4):
            stage[4 * dest + b] = total(4 * dest + b).astype(BF16)

    def g_put(src, dst, sem, device):
        remote(src, dst, g_send.at[0 if sem < 4 else 1], g_recv.at[sem], device).start()

    def edges(first, n):
        def chunk(i, carry):
            for j in range(CHUNK):
                t = i * CHUNK + j
                keep = mask[t] * table[2, 0, t] != 0
                scores = lax.dot_general(
                    hbuf[table[0, 0, t]],
                    xbuf[table[1, 0, t]],
                    (((1,), (1,)), ((), ())),
                    preferred_element_type=F32,
                )
                edge_grad[t] = jnp.where(keep, scores, 0.0).astype(BF16)
            return carry

        lax.fori_loop(first // CHUNK, (first + n) // CHUNK, chunk, 0)

    sides = ((1, 0), (-1, 1))
    for q in (1, 0):
        dest = row_of((yh + q) % 2, x + 2)
        fill(dest)
        for s, half in sides:
            i = 2 * q + half
            g_put(
                stage.at[pl.ds(4 * dest + 2 * half, 2)],
                relayed.at[pl.ds(2 * i, 2)],
                i,
                to_row[0, s],
            )
    dest = row_of(1 - yh, x)
    fill(dest)
    g_put(stage.at[pl.ds(4 * dest, 4)], landed.at[pl.ds(16, 4)], 4, to_row[1, 0])
    for q in (1, 0):
        for s, half in sides:
            fill(row_of((yh + q) % 2, x + s))
    x_got(0, 0, 8, 5)
    edges(0, slots // 4)
    part = stage.at[pl.ds(0, 8)]
    remote(part, part, g_send.at[0], g_recv.at[0], to_core).wait_send()
    for q in (1, 0):
        for s, half in sides:
            dest = row_of((yh + q) % 2, x + s)
            i = 2 * q + half
            plain = 1 - half
            g_put(
                stage.at[pl.ds(4 * dest + 2 * plain, 2)],
                landed.at[pl.ds(4 * i + 2 * plain, 2)],
                4,
                to_row[q, s],
            )
    edges(slots // 4, slots // 4)
    for q in (1, 0):
        for s, half in sides:
            dest = row_of((yh + q) % 2, x + s)
            i = 2 * q + half
            into = relayed.at[pl.ds(2 * i, 2)]
            remote(into, into, g_send.at[0], g_recv.at[i], to_core).wait_recv()
            for b in (0, 1):
                merged[2 * i + b] = (
                    total(4 * dest + 2 * half + b) + relayed[2 * i + b].astype(F32)
                ).astype(BF16)
            g_put(
                merged.at[pl.ds(2 * i, 2)],
                landed.at[pl.ds(4 * i + 2 * half, 2)],
                4,
                to_row[q, s],
            )
    edges(slots // 2, slots // 2)
    remote(landed, landed, g_send.at[0], g_recv.at[4], to_core).wait_recv()
    for b in range(4):
        value = total(4 * r + b)
        for i in range(5):
            value += landed[4 * i + b].astype(F32)
        feature_grad[b] = value.astype(BF16)

    part = hbuf.at[pl.ds(0, sum(sent))]
    remote(part, part, h_send.at[0], h_recv.at[0], to_core).wait_send()
    part = xbuf.at[pl.ds(0, 28)]
    remote(part, part, x_send.at[0], x_recv.at[0], to_core).wait_send()
    remote(landed, landed, g_send.at[1], g_recv.at[0], to_core).wait_send()


def local(features, weight, out_grad, tile_index, edge_mask, edge_weight):
    nodes, width = features.shape
    slots = edge_mask.shape[2]
    table = tile_index[0].transpose(2, 0, 1)
    blocks = nodes // BLOCK
    rows, cols = 4 * 4 * NZ, 4 * 2 * NX
    vmem = pl.BlockSpec(memory_space=pltpu.VMEM)
    hbm = pl.BlockSpec(memory_space=pl.ANY)
    dma = pltpu.SemaphoreType.DMA
    tile = (BLOCK, BLOCK)

    edge_grad, feature_grad = pl.pallas_call(
        kernel,
        in_specs=[pl.BlockSpec(memory_space=pltpu.SMEM), vmem, vmem, vmem, hbm, hbm, hbm],
        out_specs=[vmem, vmem],
        out_shape=[pltpu.VMEM((slots, *tile), BF16), pltpu.VMEM((blocks, *tile), BF16)],
        scratch_shapes=[
            pltpu.VMEM((rows, *tile), BF16),
            pltpu.VMEM((cols, *tile), BF16),
            pltpu.VMEM((slots, *tile), jnp.int32),
            pltpu.VMEM((slots, *tile), BF16),
            pltpu.VMEM((slots, *tile), BF16),
            pltpu.VMEM((slots + 1, *tile), F32),
            pltpu.VMEM((cols, *tile), BF16),
            pltpu.VMEM((8, *tile), BF16),
            pltpu.VMEM((8, *tile), BF16),
            pltpu.VMEM((20, *tile), BF16),
            pltpu.VMEM((8, 128), jnp.int32),
            pltpu.SMEM((8, 128), jnp.int32),
            dma((4,)),
            dma((1,)),
            dma((53,)),
            dma((1,)),
            dma((6,)),
            dma((2,)),
            dma((5,)),
        ],
        compiler_params=pltpu.CompilerParams(
            collective_id=0, has_side_effects=True, vmem_limit_bytes=56 << 20
        ),
        name="layer",
    )(
        table,
        table,
        out_grad,
        weight,
        features.reshape(blocks, *tile),
        edge_mask[0, 0],
        edge_weight[0, 0],
    )
    return (edge_grad[None, None], feature_grad.reshape(nodes, width))


def solution(mesh):
    in_specs = (
        P(("col", "row"), None),
        P(),
        P(("row", "col"), None),
        P("row", "col", None, None),
        P("row", "col", None, None, None),
        P("row", "col", None, None, None),
    )
    out_specs = (P("row", "col", None, None, None), P(("col", "row"), None))
    return jax.shard_map(local, mesh=mesh, in_specs=in_specs, out_specs=out_specs, check_vma=False)
```

```python
import jax
import jax.numpy as jnp
from jax import lax
from jax.experimental import pallas as pl
from jax.experimental.pallas import tpu as pltpu
from jax.sharding import PartitionSpec as P

MESH = pl.DeviceIdType.MESH
BLOCK = 128
NX, NZ = 4, 8
CHUNK, GROUP = 8, 32
F32, BF16 = jnp.float32, jnp.bfloat16
RIDE, POST = (0, 1), (2, 3)


def kernel(
    table,
    table_v,
    out_grad,
    weight,
    features,
    edge_mask,
    edge_weight,
    edge_grad,
    feature_grad,
    hbuf,
    xbuf,
    mask,
    wts,
    adj,
    sums,
    stage,
    merged,
    relayed,
    landed,
    order_v,
    order,
    load_sem,
    h_send,
    h_recv,
    x_send,
    x_recv,
    g_send,
    g_recv,
):
    slots = mask.shape[0]
    r, c = lax.axis_index("row"), lax.axis_index("col")
    yh, x = r // NX, r % NX
    yl, z, k = c // (2 * NZ), (c // 2) % NZ, c % 2

    def col_of(yl, z, k):
        return (yl * NZ + (z + NZ) % NZ) * 2 + k

    def row_of(yh, x):
        return yh * NX + (x + NX) % NX

    to_z = {s: (r, col_of(yl, z + s, k)) for s in (1, -1)}
    to_y = (r, col_of(1 - yl, z, k))
    to_core = (r, col_of(yl, z, 1 - k))
    to_row = {
        (q, s): (row_of((yh + q) % 2, x + s), c)
        for q in (0, 1)
        for s in (-1, 0, 1)
        if q or s
    }

    loads = [
        pltpu.make_async_copy(src, dst, load_sem.at[i])
        for i, (src, dst) in enumerate(
            ((features, xbuf.at[pl.ds(4 * r, 4)]), (edge_mask, mask), (edge_weight, wts))
        )
    ]
    for load in loads:
        load.start()

    barrier = pltpu.get_barrier_semaphore()
    peers = [to_z[1], to_z[-1], to_y, to_core, *to_row.values()]
    for peer in peers:
        pl.semaphore_signal(barrier, inc=1, device_id=peer, device_id_type=MESH)

    folded = lax.dot_general(
        out_grad[...], weight[...], (((1,), (1,)), ((), ())), preferred_element_type=F32
    ).astype(BF16)
    for b in range(4):
        hbuf[4 * c + b] = folded[b * BLOCK : (b + 1) * BLOCK]
    pl.semaphore_wait(barrier, len(peers))

    def remote(src, dst, send_sem, recv_sem, device):
        return pltpu.make_async_remote_copy(
            src_ref=src,
            dst_ref=dst,
            send_sem=send_sem,
            recv_sem=recv_sem,
            device_id=device,
            device_id_type=MESH,
        )

    names = [("mate", b) for b in RIDE]
    names += [("near", s, sign, b) for s in (1, 2, 3) for sign in (1, -1) for b in (*RIDE, *POST)]
    names += [("near", 4, 1, b) for b in (*RIDE, *POST)]
    names += [("far", s, sign, b) for s in (1, 2, 3) for sign in (1, -1) for b in RIDE]
    names += [("far", 4, 1, b) for b in RIDE]
    names += [("late", s) for s in (0, 1, -1, 2, -2, 3, -3, 4)]
    names += [("core",)]
    h_sem = {name: i for i, name in enumerate(names)}

    sent = []

    def put(block, first, n, device, *name):
        piece = hbuf.at[pl.ds(4 * block + first, n)]
        remote(piece, piece, h_send.at[0], h_recv.at[h_sem[name]], device).start()
        sent.append(n)

    def got(block, first, n, *name):
        piece = hbuf.at[pl.ds(4 * block + first, n)]
        remote(piece, piece, h_send.at[0], h_recv.at[h_sem[name]], to_core).wait_recv()

    def put_core(block):
        put(block, 0, 4, to_core, "core")

    def x_put(block, first, n, device, sem):
        piece = xbuf.at[pl.ds(4 * block + first, n)]
        remote(piece, piece, x_send.at[0], x_recv.at[sem], device).start()

    def x_got(block, first, n, sem):
        piece = xbuf.at[pl.ds(4 * block + first, n)]
        remote(piece, piece, x_send.at[0], x_recv.at[sem], to_core).wait_recv()

    for b in RIDE:
        put(c, b, 1, to_y, "mate", b)
    for b in (*RIDE, *POST):
        for sign in (1, -1):
            put(c, b, 1, to_z[sign], "near", 1, sign, b)
    for b in POST:
        put(c, b, 1, to_y, "late", 0)
    put_core(c)
    loads[0].wait()
    x_put(r, 0, 4, to_row[0, 1], 1)
    x_put(r, 0, 4, to_row[0, -1], 2)

    square = (slots, slots)
    at_s = lax.broadcasted_iota(jnp.int32, square, 0)
    at_q = lax.broadcasted_iota(jnp.int32, square, 1)

    def upright(line):
        return jnp.sum(
            jnp.where(at_s == at_q, jnp.broadcast_to(line, square), 0), axis=1, keepdims=True
        )

    def gather(where, column):
        return jnp.sum(jnp.where(where, column, 0), axis=0, keepdims=True)

    cols = jnp.broadcast_to(table_v[1], square)
    col_up, row_up = upright(table_v[1]), upright(table_v[0])
    before = cols * slots + at_q < col_up * slots + at_s
    rank = jnp.sum(jnp.where(before, 1, 0), axis=1, keepdims=True)
    here = rank == at_q
    col_here = gather(here, col_up)
    col_before = gather(rank == at_q - 1, col_up)
    first_lane = at_q[0:1] == 0
    order_v[0:1, 0:slots] = gather(here, at_s)
    order_v[1:2, 0:slots] = gather(here, row_up)
    order_v[2:3, 0:slots] = jnp.where((col_here == col_before) & ~first_lane, 1, 0)
    order_v[3:4, 0:slots] = jnp.where(
        gather(col_up == at_q, 1) > 0, gather(col_up <= at_q, 1) - 1, -1
    )
    to_scalar = pltpu.make_async_copy(order_v, order, load_sem.at[3])
    to_scalar.start()
    mate = col_of(1 - yl, z, k)
    for b in RIDE:
        got(mate, b, 1, "mate", b)
        for sign in (1, -1):
            put(mate, b, 1, to_z[sign], "far", 1, sign, b)
    to_scalar.wait()
    loads[1].wait()
    loads[2].wait()

    def prepare(first, n):
        def one(i, carry):
            t = order[0, i]
            keep = mask[t] * table[2, 0, t] != 0
            kept = jnp.where(keep, wts[t].astype(F32), 0.0)
            adj[i] = kept.T.astype(BF16)
            return carry

        lax.fori_loop(first, first + n, one, 0, unroll=2)

    def late(s):
        block = col_of(1 - yl, z + s, k)
        got(block, POST[0], len(POST), "late", s)
        put_core(block)

    prepare(0, 8)
    done = 8
    for s in (1, 2, 3):
        near = {sign: col_of(yl, z - sign * s, k) for sign in (1, -1)}
        far = {sign: col_of(1 - yl, z - sign * s, k) for sign in (1, -1)}
        for b in (*RIDE, *POST):
            for sign in (1, -1):
                got(near[sign], b, 1, "near", s, sign, b)
                if s < 3:
                    put(near[sign], b, 1, to_z[sign], "near", s + 1, sign, b)
                elif b in ((0, 1) if sign > 0 else (2, 3)):
                    put(near[sign], b, 1, to_z[sign], "near", 4, 1, b)
                if b in POST:
                    put(near[sign], b, 1, to_y, "late", -sign * s)
        for sign in (1, -1):
            put_core(near[sign])
        for b in RIDE:
            for sign in (1, -1):
                got(far[sign], b, 1, "far", s, sign, b)
                if s < 3:
                    put(far[sign], b, 1, to_z[sign], "far", s + 1, sign, b)
            if s == 3:
                way = 1 - 2 * k
                put(
                    col_of(1 - yl, z - 3 * way, k),
                    b,
                    1,
                    (r, col_of(yl, z + way, k)),
                    "far",
                    4,
                    1,
                    b,
                )
        for back in (s - 1,) if s == 1 else (s - 1, 1 - s):
            late(back)
        if s == 1:
            x_put(r, 0, 4, to_row[1, 0], 0)
        if s == 2:
            left, right = row_of(yh, x - 1), row_of(yh, x + 1)
            x_got(left, 0, 4, 1)
            x_put(left, 0, 2, to_row[0, 1], 5)
            x_got(right, 0, 4, 2)
            x_put(right, 2, 2, to_row[0, -1], 5)
        if s == 3:
            other = row_of(1 - yh, x)
            x_got(other, 0, 4, 0)
            x_put(other, 0, 4, to_row[0, 1], 3)
            x_put(other, 0, 4, to_row[0, -1], 4)
        more = 24 if s < 3 else slots - done
        if more:
            prepare(done, more)
        done += more
    near, far = col_of(yl, z + 4, k), col_of(1 - yl, z + 4, k)
    for b in POST:
        got(near, b, 1, "near", 4, 1, b)
        put(near, b, 1, to_y, "late", 4)
    for b in RIDE:
        got(near, b, 1, "near", 4, 1, b)
    put_core(near)
    for b in RIDE:
        got(far, b, 1, "far", 4, 1, b)
    for s in (3, -3, 4):
        late(s)
    left, right = row_of(1 - yh, x - 1), row_of(1 - yh, x + 1)
    x_got(left, 0, 4, 3)
    x_put(left, 0, 2, to_row[0, 1], 5)
    x_got(right, 0, 4, 4)
    x_put(right, 2, 2, to_row[0, -1], 5)
    got(0, 0, 8 * NZ, "core")

    def group(g, carry):
        run = sums[g * GROUP]
        for j in range(GROUP):
            i = g * GROUP + j
            added = jnp.dot(adj[i], hbuf[order[1, i]], preferred_element_type=F32)
            run = added + jnp.where(order[2, i] != 0, run, 0.0)
            sums[i + 1] = run
        return carry

    sums[0] = jnp.zeros((BLOCK, BLOCK), F32)
    lax.fori_loop(0, slots // GROUP, group, 0)

    def total(block):
        at = order[3, block]
        return jnp.where(at >= 0, sums[at + 1], 0.0)

    def fill(dest):
        for b in range(4):
            stage[4 * dest + b] = total(4 * dest + b).astype(BF16)

    def g_put(src, dst, sem, device):
        remote(src, dst, g_send.at[0 if sem < 8 else 1], g_recv.at[sem], device).start()

    def edges(first, n):
        def chunk(i, carry):
            for j in range(CHUNK):
                t = i * CHUNK + j
                keep = mask[t] * table[2, 0, t] != 0
                scores = lax.dot_general(
                    hbuf[table[0, 0, t]],
                    xbuf[table[1, 0, t]],
                    (((1,), (1,)), ((), ())),
                    preferred_element_type=F32,
                )
                edge_grad[t] = jnp.where(keep, scores, 0.0).astype(BF16)
            return carry

        lax.fori_loop(first // CHUNK, (first + n) // CHUNK, chunk, 0)

    sides = ((1, 0), (-1, 1))
    for q in (1, 0):
        dest = row_of((yh + q) % 2, x + 2)
        fill(dest)
        for s, half in sides:
            i = 2 * q + half
            for p in (0, 1):
                g_put(
                    stage.at[pl.ds(4 * dest + 2 * half + p, 1)],
                    relayed.at[pl.ds(2 * i + p, 1)],
                    2 * i + p,
                    to_row[0, s],
                )
    dest = row_of(1 - yh, x)
    fill(dest)
    g_put(stage.at[pl.ds(4 * dest, 4)], landed.at[pl.ds(16, 4)], 8, to_row[1, 0])
    for q in (1, 0):
        for s, half in sides:
            fill(row_of((yh + q) % 2, x + s))
    x_got(0, 0, 8, 5)
    edges(0, slots // 4)
    for q in (1, 0):
        for s, half in sides:
            dest = row_of((yh + q) % 2, x + s)
            i = 2 * q + half
            plain = 1 - half
            g_put(
                stage.at[pl.ds(4 * dest + 2 * plain, 2)],
                landed.at[pl.ds(4 * i + 2 * plain, 2)],
                8,
                to_row[q, s],
            )
    edges(slots // 4, slots // 4)
    for q in (1, 0):
        for s, half in sides:
            dest = row_of((yh + q) % 2, x + s)
            i = 2 * q + half
            for p in (0, 1):
                into = relayed.at[pl.ds(2 * i + p, 1)]
                remote(into, into, g_send.at[0], g_recv.at[2 * i + p], to_core).wait_recv()
                merged[2 * i + p] = (
                    total(4 * dest + 2 * half + p) + relayed[2 * i + p].astype(F32)
                ).astype(BF16)
                g_put(
                    merged.at[pl.ds(2 * i + p, 1)],
                    landed.at[pl.ds(4 * i + 2 * half + p, 1)],
                    8,
                    to_row[q, s],
                )
    edges(slots // 2, slots // 2)
    remote(landed, landed, g_send.at[0], g_recv.at[8], to_core).wait_recv()
    for b in range(4):
        value = total(4 * r + b)
        for i in range(5):
            value += landed[4 * i + b].astype(F32)
        feature_grad[b] = value.astype(BF16)

    part = hbuf.at[pl.ds(0, sum(sent))]
    remote(part, part, h_send.at[0], h_recv.at[0], to_core).wait_send()
    part = xbuf.at[pl.ds(0, 28)]
    remote(part, part, x_send.at[0], x_recv.at[0], to_core).wait_send()
    remote(landed, landed, g_send.at[1], g_recv.at[0], to_core).wait_send()
    part = stage.at[pl.ds(0, 8)]
    remote(part, part, g_send.at[0], g_recv.at[0], to_core).wait_send()


def write(edges, grads, edges_out, grads_out, sem):
    copies = [
        pltpu.make_async_copy(edges, edges_out, sem.at[0]),
        pltpu.make_async_copy(grads, grads_out, sem.at[1]),
    ]
    for copy in copies:
        copy.start()
    for copy in copies:
        copy.wait()


def local(features, weight, out_grad, tile_index, edge_mask, edge_weight):
    nodes, width = features.shape
    slots = edge_mask.shape[2]
    table = tile_index[0].transpose(2, 0, 1)
    blocks = nodes // BLOCK
    rows, cols = 4 * 4 * NZ, 4 * 2 * NX
    vmem = pl.BlockSpec(memory_space=pltpu.VMEM)
    hbm = pl.BlockSpec(memory_space=pl.ANY)
    dma = pltpu.SemaphoreType.DMA
    tile = (BLOCK, BLOCK)

    edge_grad, feature_grad = pl.pallas_call(
        kernel,
        in_specs=[pl.BlockSpec(memory_space=pltpu.SMEM), vmem, vmem, vmem, hbm, hbm, hbm],
        out_specs=[vmem, vmem],
        out_shape=[pltpu.VMEM((slots, *tile), BF16), pltpu.VMEM((blocks, *tile), BF16)],
        scratch_shapes=[
            pltpu.VMEM((rows, *tile), BF16),
            pltpu.VMEM((cols, *tile), BF16),
            pltpu.VMEM((slots, *tile), jnp.int32),
            pltpu.VMEM((slots, *tile), BF16),
            pltpu.VMEM((slots, *tile), BF16),
            pltpu.VMEM((slots + 1, *tile), F32),
            pltpu.VMEM((cols, *tile), BF16),
            pltpu.VMEM((8, *tile), BF16),
            pltpu.VMEM((8, *tile), BF16),
            pltpu.VMEM((20, *tile), BF16),
            pltpu.VMEM((8, 128), jnp.int32),
            pltpu.SMEM((8, 128), jnp.int32),
            dma((4,)),
            dma((1,)),
            dma((53,)),
            dma((1,)),
            dma((6,)),
            dma((2,)),
            dma((9,)),
        ],
        compiler_params=pltpu.CompilerParams(
            collective_id=0, has_side_effects=True, vmem_limit_bytes=56 << 20
        ),
        name="layer",
    )(
        table,
        table,
        out_grad,
        weight,
        features.reshape(blocks, *tile),
        edge_mask[0, 0],
        edge_weight[0, 0],
    )
    edge_grad = pltpu.with_memory_space_constraint(edge_grad, pltpu.VMEM)
    feature_grad = pltpu.with_memory_space_constraint(feature_grad, pltpu.VMEM)
    edge_grad, feature_grad = pl.pallas_call(
        write,
        in_specs=[vmem, vmem],
        out_specs=[hbm, hbm],
        out_shape=[
            jax.ShapeDtypeStruct(edge_grad.shape, BF16),
            jax.ShapeDtypeStruct(feature_grad.shape, BF16),
        ],
        scratch_shapes=[dma((2,))],
        name="write",
    )(edge_grad, feature_grad)
    return (edge_grad[None, None], feature_grad.reshape(nodes, width))


def solution(mesh):
    in_specs = (
        P(("col", "row"), None),
        P(),
        P(("row", "col"), None),
        P("row", "col", None, None),
        P("row", "col", None, None, None),
        P("row", "col", None, None, None),
    )
    out_specs = (P("row", "col", None, None, None), P(("col", "row"), None))
    return jax.shard_map(local, mesh=mesh, in_specs=in_specs, out_specs=out_specs, check_vma=False)
```

```python
import jax
import jax.numpy as jnp
from jax import lax
from jax.experimental import pallas as pl
from jax.experimental.pallas import tpu as pltpu
from jax.sharding import PartitionSpec as P

MESH = pl.DeviceIdType.MESH
BLOCK = 128
NX, NZ = 4, 8
CHUNK, GROUP = 8, 64
F32, BF16 = jnp.float32, jnp.bfloat16
RIDE, POST = (0, 1), (2, 3)


def kernel(
    table,
    table_v,
    out_grad,
    weight,
    features,
    edge_mask,
    edge_weight,
    edge_grad,
    feature_grad,
    hbuf,
    xbuf,
    mask,
    wts,
    adj,
    sums,
    stage,
    merged,
    relayed,
    landed,
    order_v,
    order,
    load_sem,
    h_send,
    h_recv,
    x_send,
    x_recv,
    g_send,
    g_recv,
):
    slots = mask.shape[0]
    r, c = lax.axis_index("row"), lax.axis_index("col")
    yh, x = r // NX, r % NX
    yl, z, k = c // (2 * NZ), (c // 2) % NZ, c % 2

    def col_of(yl, z, k):
        return (yl * NZ + (z + NZ) % NZ) * 2 + k

    def row_of(yh, x):
        return yh * NX + (x + NX) % NX

    to_z = {s: (r, col_of(yl, z + s, k)) for s in (1, -1)}
    to_y = (r, col_of(1 - yl, z, k))
    to_core = (r, col_of(yl, z, 1 - k))
    to_row = {
        (q, s): (row_of((yh + q) % 2, x + s), c)
        for q in (0, 1)
        for s in (-1, 0, 1)
        if q or s
    }

    loads = [
        pltpu.make_async_copy(src, dst, load_sem.at[i])
        for i, (src, dst) in enumerate(
            ((features, xbuf.at[pl.ds(4 * r, 4)]), (edge_mask, mask), (edge_weight, wts))
        )
    ]
    for load in loads:
        load.start()

    barrier = pltpu.get_barrier_semaphore()
    peers = [to_z[1], to_z[-1], to_y, to_core, *to_row.values()]
    for peer in peers:
        pl.semaphore_signal(barrier, inc=1, device_id=peer, device_id_type=MESH)

    folded = lax.dot_general(
        out_grad[...], weight[...], (((1,), (1,)), ((), ())), preferred_element_type=F32
    ).astype(BF16)
    for b in range(4):
        hbuf[4 * c + b] = folded[b * BLOCK : (b + 1) * BLOCK]
    pl.semaphore_wait(barrier, len(peers))

    def remote(src, dst, send_sem, recv_sem, device):
        return pltpu.make_async_remote_copy(
            src_ref=src,
            dst_ref=dst,
            send_sem=send_sem,
            recv_sem=recv_sem,
            device_id=device,
            device_id_type=MESH,
        )

    names = [("mate", b) for b in RIDE]
    names += [("near", s, sign, b) for s in (1, 2, 3) for sign in (1, -1) for b in (*RIDE, *POST)]
    names += [("near", 4, 1, b) for b in (*RIDE, *POST)]
    names += [("far", s, sign, b) for s in (1, 2, 3) for sign in (1, -1) for b in RIDE]
    names += [("far", 4, 1, b) for b in RIDE]
    names += [("late", s) for s in (0, 1, -1, 2, -2, 3, -3, 4)]
    names += [("core",)]
    h_sem = {name: i for i, name in enumerate(names)}

    sent = []

    def put(block, first, n, device, *name):
        piece = hbuf.at[pl.ds(4 * block + first, n)]
        remote(piece, piece, h_send.at[0], h_recv.at[h_sem[name]], device).start()
        sent.append(n)

    def got(block, first, n, *name):
        piece = hbuf.at[pl.ds(4 * block + first, n)]
        remote(piece, piece, h_send.at[0], h_recv.at[h_sem[name]], to_core).wait_recv()

    def put_core(block):
        put(block, 0, 4, to_core, "core")

    def x_put(block, first, n, device, sem):
        piece = xbuf.at[pl.ds(4 * block + first, n)]
        remote(piece, piece, x_send.at[0], x_recv.at[sem], device).start()

    def x_got(block, first, n, sem):
        piece = xbuf.at[pl.ds(4 * block + first, n)]
        remote(piece, piece, x_send.at[0], x_recv.at[sem], to_core).wait_recv()

    for b in RIDE:
        put(c, b, 1, to_y, "mate", b)
    for b in (*RIDE, *POST):
        for sign in (1, -1):
            put(c, b, 1, to_z[sign], "near", 1, sign, b)
    for b in POST:
        put(c, b, 1, to_y, "late", 0)
    put_core(c)
    loads[0].wait()
    x_put(r, 0, 4, to_row[0, 1], 1)
    x_put(r, 0, 4, to_row[0, -1], 2)

    square = (slots, slots)
    at_s = lax.broadcasted_iota(jnp.int32, square, 0)
    at_q = lax.broadcasted_iota(jnp.int32, square, 1)

    def upright(line):
        return jnp.sum(
            jnp.where(at_s == at_q, jnp.broadcast_to(line, square), 0), axis=1, keepdims=True
        )

    def gather(where, column):
        return jnp.sum(jnp.where(where, column, 0), axis=0, keepdims=True)

    cols = jnp.broadcast_to(table_v[1], square)
    col_up, row_up = upright(table_v[1]), upright(table_v[0])
    before = cols * slots + at_q < col_up * slots + at_s
    rank = jnp.sum(jnp.where(before, 1, 0), axis=1, keepdims=True)
    here = rank == at_q
    col_here = gather(here, col_up)
    col_before = gather(rank == at_q - 1, col_up)
    first_lane = at_q[0:1] == 0
    order_v[0:1, 0:slots] = gather(here, at_s)
    order_v[1:2, 0:slots] = gather(here, row_up)
    order_v[2:3, 0:slots] = jnp.where((col_here == col_before) & ~first_lane, 1, 0)
    order_v[3:4, 0:slots] = jnp.where(
        gather(col_up == at_q, 1) > 0, gather(col_up <= at_q, 1) - 1, -1
    )
    to_scalar = pltpu.make_async_copy(order_v, order, load_sem.at[3])
    to_scalar.start()
    mate = col_of(1 - yl, z, k)
    for b in RIDE:
        got(mate, b, 1, "mate", b)
        for sign in (1, -1):
            put(mate, b, 1, to_z[sign], "far", 1, sign, b)
    to_scalar.wait()
    loads[1].wait()
    loads[2].wait()

    def prepare(first, n):
        def one(i, carry):
            t = order[0, i]
            keep = mask[t] * table[2, 0, t] != 0
            kept = jnp.where(keep, wts[t].astype(F32), 0.0)
            adj[i] = kept.T.astype(BF16)
            return carry

        lax.fori_loop(first, first + n, one, 0, unroll=2)

    def late(s):
        block = col_of(1 - yl, z + s, k)
        got(block, POST[0], len(POST), "late", s)
        put_core(block)

    prepare(0, 8)
    done = 8
    for s in (1, 2, 3):
        near = {sign: col_of(yl, z - sign * s, k) for sign in (1, -1)}
        far = {sign: col_of(1 - yl, z - sign * s, k) for sign in (1, -1)}
        for b in (*RIDE, *POST):
            for sign in (1, -1):
                got(near[sign], b, 1, "near", s, sign, b)
                if s < 3:
                    put(near[sign], b, 1, to_z[sign], "near", s + 1, sign, b)
                elif b in ((0, 1) if sign > 0 else (2, 3)):
                    put(near[sign], b, 1, to_z[sign], "near", 4, 1, b)
                if b in POST:
                    put(near[sign], b, 1, to_y, "late", -sign * s)
        for sign in (1, -1):
            put_core(near[sign])
        for b in RIDE:
            for sign in (1, -1):
                got(far[sign], b, 1, "far", s, sign, b)
                if s < 3:
                    put(far[sign], b, 1, to_z[sign], "far", s + 1, sign, b)
            if s == 3:
                way = 1 - 2 * k
                put(
                    col_of(1 - yl, z - 3 * way, k),
                    b,
                    1,
                    (r, col_of(yl, z + way, k)),
                    "far",
                    4,
                    1,
                    b,
                )
        for back in (s - 1,) if s == 1 else (s - 1, 1 - s):
            late(back)
        if s == 1:
            x_put(r, 0, 4, to_row[1, 0], 0)
        if s == 2:
            left, right = row_of(yh, x - 1), row_of(yh, x + 1)
            x_got(left, 0, 4, 1)
            x_put(left, 0, 2, to_row[0, 1], 5)
            x_got(right, 0, 4, 2)
            x_put(right, 2, 2, to_row[0, -1], 5)
        if s == 3:
            other = row_of(1 - yh, x)
            x_got(other, 0, 4, 0)
            x_put(other, 0, 4, to_row[0, 1], 3)
            x_put(other, 0, 4, to_row[0, -1], 4)
        more = 24 if s < 3 else slots - done
        if more:
            prepare(done, more)
        done += more
    near, far = col_of(yl, z + 4, k), col_of(1 - yl, z + 4, k)
    for b in POST:
        got(near, b, 1, "near", 4, 1, b)
        put(near, b, 1, to_y, "late", 4)
    for b in RIDE:
        got(near, b, 1, "near", 4, 1, b)
    put_core(near)
    for b in RIDE:
        got(far, b, 1, "far", 4, 1, b)
    for s in (3, -3, 4):
        late(s)
    left, right = row_of(1 - yh, x - 1), row_of(1 - yh, x + 1)
    x_got(left, 0, 4, 3)
    x_put(left, 0, 2, to_row[0, 1], 5)
    x_got(right, 0, 4, 4)
    x_put(right, 2, 2, to_row[0, -1], 5)
    got(0, 0, 8 * NZ, "core")

    def group(g, carry):
        run = sums[g * GROUP]
        for j in range(GROUP):
            i = g * GROUP + j
            added = jnp.dot(adj[i], hbuf[order[1, i]], preferred_element_type=F32)
            run = added + jnp.where(order[2, i] != 0, run, 0.0)
            sums[i + 1] = run
        return carry

    sums[0] = jnp.zeros((BLOCK, BLOCK), F32)
    lax.fori_loop(0, slots // GROUP, group, 0)

    def total(block):
        at = order[3, block]
        return jnp.where(at >= 0, sums[at + 1], 0.0)

    def fill(dest):
        for b in range(4):
            stage[4 * dest + b] = total(4 * dest + b).astype(BF16)

    def g_put(src, dst, sem, device):
        remote(src, dst, g_send.at[0 if sem < 8 else 1], g_recv.at[sem], device).start()

    def edges(first, n):
        def chunk(i, carry):
            for j in range(CHUNK):
                t = i * CHUNK + j
                keep = mask[t] * table[2, 0, t] != 0
                scores = lax.dot_general(
                    hbuf[table[0, 0, t]],
                    xbuf[table[1, 0, t]],
                    (((1,), (1,)), ((), ())),
                    preferred_element_type=F32,
                )
                edge_grad[t] = jnp.where(keep, scores, 0.0).astype(BF16)
            return carry

        lax.fori_loop(first // CHUNK, (first + n) // CHUNK, chunk, 0)

    sides = ((1, 0), (-1, 1))
    for q in (1, 0):
        dest = row_of((yh + q) % 2, x + 2)
        fill(dest)
        for s, half in sides:
            i = 2 * q + half
            for p in (0, 1):
                g_put(
                    stage.at[pl.ds(4 * dest + 2 * half + p, 1)],
                    relayed.at[pl.ds(2 * i + p, 1)],
                    2 * i + p,
                    to_row[0, s],
                )
    dest = row_of(1 - yh, x)
    fill(dest)
    g_put(stage.at[pl.ds(4 * dest, 4)], landed.at[pl.ds(16, 4)], 8, to_row[1, 0])
    for q in (1, 0):
        for s, half in sides:
            fill(row_of((yh + q) % 2, x + s))
    x_got(0, 0, 8, 5)
    edges(0, slots // 4)
    for q in (1, 0):
        for s, half in sides:
            dest = row_of((yh + q) % 2, x + s)
            i = 2 * q + half
            plain = 1 - half
            g_put(
                stage.at[pl.ds(4 * dest + 2 * plain, 2)],
                landed.at[pl.ds(4 * i + 2 * plain, 2)],
                8,
                to_row[q, s],
            )
    edges(slots // 4, slots // 4)
    for q in (1, 0):
        for s, half in sides:
            dest = row_of((yh + q) % 2, x + s)
            i = 2 * q + half
            for p in (0, 1):
                into = relayed.at[pl.ds(2 * i + p, 1)]
                remote(into, into, g_send.at[0], g_recv.at[2 * i + p], to_core).wait_recv()
                merged[2 * i + p] = (
                    total(4 * dest + 2 * half + p) + relayed[2 * i + p].astype(F32)
                ).astype(BF16)
                g_put(
                    merged.at[pl.ds(2 * i + p, 1)],
                    landed.at[pl.ds(4 * i + 2 * half + p, 1)],
                    8,
                    to_row[q, s],
                )
    edges(slots // 2, slots // 2)
    remote(landed, landed, g_send.at[0], g_recv.at[8], to_core).wait_recv()
    for b in range(4):
        value = total(4 * r + b)
        for i in range(5):
            value += landed[4 * i + b].astype(F32)
        feature_grad[b] = value.astype(BF16)

    part = hbuf.at[pl.ds(0, sum(sent))]
    remote(part, part, h_send.at[0], h_recv.at[0], to_core).wait_send()
    part = xbuf.at[pl.ds(0, 28)]
    remote(part, part, x_send.at[0], x_recv.at[0], to_core).wait_send()
    remote(landed, landed, g_send.at[1], g_recv.at[0], to_core).wait_send()
    part = stage.at[pl.ds(0, 8)]
    remote(part, part, g_send.at[0], g_recv.at[0], to_core).wait_send()


def write(edges, grads, edges_out, grads_out, sem):
    copies = [
        pltpu.make_async_copy(edges, edges_out, sem.at[0]),
        pltpu.make_async_copy(grads, grads_out, sem.at[1]),
    ]
    for copy in copies:
        copy.start()
    for copy in copies:
        copy.wait()


def local(features, weight, out_grad, tile_index, edge_mask, edge_weight):
    nodes, width = features.shape
    slots = edge_mask.shape[2]
    table = tile_index[0].transpose(2, 0, 1)
    blocks = nodes // BLOCK
    rows, cols = 4 * 4 * NZ, 4 * 2 * NX
    vmem = pl.BlockSpec(memory_space=pltpu.VMEM)
    hbm = pl.BlockSpec(memory_space=pl.ANY)
    dma = pltpu.SemaphoreType.DMA
    tile = (BLOCK, BLOCK)

    edge_grad, feature_grad = pl.pallas_call(
        kernel,
        in_specs=[pl.BlockSpec(memory_space=pltpu.SMEM), vmem, vmem, vmem, hbm, hbm, hbm],
        out_specs=[vmem, vmem],
        out_shape=[pltpu.VMEM((slots, *tile), BF16), pltpu.VMEM((blocks, *tile), BF16)],
        scratch_shapes=[
            pltpu.VMEM((rows, *tile), BF16),
            pltpu.VMEM((cols, *tile), BF16),
            pltpu.VMEM((slots, *tile), jnp.int32),
            pltpu.VMEM((slots, *tile), BF16),
            pltpu.VMEM((slots, *tile), BF16),
            pltpu.VMEM((slots + 1, *tile), F32),
            pltpu.VMEM((cols, *tile), BF16),
            pltpu.VMEM((8, *tile), BF16),
            pltpu.VMEM((8, *tile), BF16),
            pltpu.VMEM((20, *tile), BF16),
            pltpu.VMEM((8, 128), jnp.int32),
            pltpu.SMEM((8, 128), jnp.int32),
            dma((4,)),
            dma((1,)),
            dma((53,)),
            dma((1,)),
            dma((6,)),
            dma((2,)),
            dma((9,)),
        ],
        compiler_params=pltpu.CompilerParams(
            collective_id=0, has_side_effects=True, vmem_limit_bytes=56 << 20
        ),
        name="layer",
    )(
        table,
        table,
        out_grad,
        weight,
        features.reshape(blocks, *tile),
        edge_mask[0, 0],
        edge_weight[0, 0],
    )
    edge_grad = pltpu.with_memory_space_constraint(edge_grad, pltpu.VMEM)
    feature_grad = pltpu.with_memory_space_constraint(feature_grad, pltpu.VMEM)
    edge_grad, feature_grad = pl.pallas_call(
        write,
        in_specs=[vmem, vmem],
        out_specs=[hbm, hbm],
        out_shape=[
            jax.ShapeDtypeStruct(edge_grad.shape, BF16),
            jax.ShapeDtypeStruct(feature_grad.shape, BF16),
        ],
        scratch_shapes=[dma((2,))],
        name="write",
    )(edge_grad, feature_grad)
    return (edge_grad[None, None], feature_grad.reshape(nodes, width))


def solution(mesh):
    in_specs = (
        P(("col", "row"), None),
        P(),
        P(("row", "col"), None),
        P("row", "col", None, None),
        P("row", "col", None, None, None),
        P("row", "col", None, None, None),
    )
    out_specs = (P("row", "col", None, None, None), P(("col", "row"), None))
    return jax.shard_map(local, mesh=mesh, in_specs=in_specs, out_specs=out_specs, check_vma=False)
```
